32 devices in a mesh: member: 8 (over z, core), dp: 4 (over y, x).
Axes of the slice: x: 2, y: 2, z: 4, core: 2. Of those that a mesh axis runs over, the one named last changes fastest.
Arguments:
- feats: bfloat16 [8, 2048, 1024], P('member', 'dp'), may hold values from -160 to 160
- pair_weight: float32 [8, 3], replicated, may hold values from 0.5 to 2
Outputs:
- grad_centred: float32 [8, 2048, 1024], P('member', 'dp')
- cka: float32 [8, 3], P('member')
The draws below stay inside these ranges and needn't reach their ends.
All inputs are finite; a program needn't handle non-finite values.
Results may differ from the reference program's by a relative error of at most 0.0053.
Values may be sent and summed in bfloat16 or wider, within the bound.
A program may use at most 128 MiB of HBM per device.

```python
import math
import jax
import jax.numpy as jnp
from jax import lax

F = 1024
PAIRS = 3
BATCH = 2048
MEMBERS = 8


def draw_feats(key, part):
    keys = jax.random.split(jax.random.fold_in(key, 71), 4)
    shape = (MEMBERS, BATCH, F)
    noise = jnp.clip(jax.random.normal(keys[0], shape, jnp.float32), -5.0, 5.0)
    position = jnp.arange(BATCH, dtype=jnp.float32) / BATCH
    ramp = (3.0 ** position)[None, :, None] / 3.0
    row_scale = ramp * 10.0 ** jax.random.uniform(keys[1], (MEMBERS, BATCH, 1), jnp.float32, 0.0, 1.0)
    col_scale = 10.0 ** jax.random.uniform(keys[2], (MEMBERS, 1, F), jnp.float32, -0.5, 0.5)
    offset = jax.random.uniform(keys[3], (MEMBERS, 1, F), jnp.float32, -1.5, 1.5)
    return (row_scale * col_scale * noise + offset).astype(jnp.bfloat16)


def setup_inputs(seed: int = 0) -> dict:
    key_of = jax.random.split(jax.random.key(seed), 3)
    return {
        "feats": draw_feats(jax.random.fold_in(key_of[2], 71), 0),
        "pair_weight": jnp.clip(jnp.exp(jax.random.uniform(key_of[1], (MEMBERS, PAIRS), jnp.float32, math.log(0.5), math.log(2.0))), 0.5, 2.0),
    }


def reference(feats, pair_weight):
    members = feats.shape[0]
    batch = feats.shape[1]
    mean = lax.optimization_barrier(jnp.sum(feats.astype(jnp.float32), axis=1, keepdims=True)) / batch
    centred = (feats.astype(jnp.float32) - mean).astype(jnp.bfloat16)
    covs = []
    for member in range(members):
        row = []
        for offset in range(PAIRS + 1):
            partner = (member + offset) % members
            row.append(jnp.dot(centred[member].T, centred[partner], preferred_element_type=jnp.float32))
        covs.append(row)
    hself = jnp.stack([jnp.sum(covs[m][0] * covs[m][0]) for m in range(members)])
    hpair = jnp.stack([jnp.stack([jnp.sum(covs[m][o] * covs[m][o]) for o in range(1, PAIRS + 1)]) for m in range(members)])
    partner_self = jnp.stack([jnp.roll(hself, -o) for o in range(1, PAIRS + 1)], axis=1)
    norms = jnp.sqrt(hself[:, None] * partner_self)
    cka = hpair / norms
    weighted = pair_weight * cka
    mixers = []
    for member in range(members):
        mixers.append([(2.0 * pair_weight[member, o - 1] / norms[member, o - 1] * covs[member][o]).astype(jnp.bfloat16) for o in range(1, PAIRS + 1)])
    grads = []
    for member in range(members):
        incoming = jnp.float32(0.0)
        for o in range(1, PAIRS + 1):
            incoming = incoming + weighted[(member - o) % members, o - 1]
        self_coef = (jnp.sum(weighted[member]) + incoming) / (hself[member] + 1e-06)
        self_mix = (2.0 * self_coef * covs[member][0]).astype(jnp.bfloat16)
        total = -jnp.dot(centred[member], self_mix, preferred_element_type=jnp.float32)
        for o in range(1, PAIRS + 1):
            total = total + jnp.dot(centred[(member + o) % members], mixers[member][o - 1].T, preferred_element_type=jnp.float32)
            source = (member - o) % members
            total = total + jnp.dot(centred[source], mixers[source][o - 1], preferred_element_type=jnp.float32)
        grads.append(math.sqrt(batch) * total)
    return (jnp.stack(grads), cka)
```

```python
import math

import jax
import jax.numpy as jnp
from jax import lax
from jax.sharding import PartitionSpec as P


def mixing(self_hsic, pair_hsic, pair_weight):
    pairs = pair_weight.shape[1]
    members = pair_weight.shape[0]
    partner_self = jnp.stack([jnp.roll(self_hsic, -o) for o in range(1, pairs + 1)], axis=1)
    norms = jnp.sqrt(self_hsic[:, None] * partner_self)
    cka = pair_hsic / norms
    weighted = pair_weight * cka
    incoming = sum(jnp.roll(weighted[:, o - 1], o) for o in range(1, pairs + 1))
    self_coef = (jnp.sum(weighted, axis=1) + incoming) / (self_hsic + 1e-06)
    coef = 2.0 * pair_weight / norms
    eye = jnp.eye(members, dtype=jnp.float32)
    mix = -2.0 * self_coef[:, None] * eye
    for o in range(1, pairs + 1):
        ahead = coef[:, o - 1][:, None] * jnp.roll(eye, o, axis=1)
        mix = mix + ahead + ahead.T
    return cka, mix


def shards(feats, pair_weight):
    rows = feats[0]
    members = lax.axis_size("member")
    pairs = pair_weight.shape[1]
    whole = lax.all_gather(rows, "dp", axis=0, tiled=True)
    batch, width = whole.shape
    mean = jnp.sum(whole.astype(jnp.float32), axis=0) / batch
    centred = (whole.astype(jnp.float32) - mean).astype(jnp.bfloat16)
    own = (rows.astype(jnp.float32) - mean).astype(jnp.bfloat16)
    blocks = centred.reshape(members, batch // members, width)
    gram = jnp.einsum("rf,mcf->mrc", own, blocks, preferred_element_type=jnp.float32)
    held = lax.all_to_all(gram.astype(jnp.bfloat16), "member", 0, 0)
    held = held.astype(jnp.float32)
    sums = []
    for o in range(pairs + 1):
        sums.append(jnp.sum(held * jnp.roll(held, -o, axis=0), axis=(1, 2)))
    sums = lax.psum(jnp.stack(sums, axis=1), ("member", "dp"))
    cka, mix = mixing(sums[:, 0], sums[:, 1:], pair_weight)
    mixed = jnp.stack(
        [sum(mix[m, q] * held[q] for q in range(members)) for m in range(members)]
    ).astype(jnp.bfloat16)
    mixed = lax.all_to_all(mixed, "member", 0, 0)
    grad = jnp.einsum("jrc,jcf->rf", mixed, blocks, preferred_element_type=jnp.float32)
    grad = math.sqrt(batch) * grad
    own_cka = lax.dynamic_slice_in_dim(cka, lax.axis_index("member"), 1, axis=0)
    return (grad[None], own_cka)


def solution(mesh):
    return jax.shard_map(
        shards,
        mesh=mesh,
        in_specs=(P("member", "dp", None), P()),
        out_specs=(P("member", "dp", None), P("member", None)),
        check_vma=False,
    )
```

```python
import functools
import math

import jax
import jax.numpy as jnp
from jax import lax
from jax.experimental import pallas as pl
from jax.experimental.pallas import tpu as pltpu
from jax.sharding import PartitionSpec as P

MESH = pl.DeviceIdType.MESH
LANES = 128


def flipped(index, bits, count):
    place, value = 1, 0
    while place < count:
        bit = (index // place) % 2
        value = value + ((1 - bit) if bits & place else bit) * place
        place *= 2
    return value


def rolled(value, steps):
    count = value.shape[0]
    steps %= count
    if steps == 0:
        return value
    return jnp.concatenate([value[count - steps:], value[:count - steps]], axis=0)


def kernel(members, parts, pairs, x_ref, weight_ref, grad_ref, cka_ref, sums, raw, cent, gram, held,
           mixed, back, acc, stage, coefs, sum_send, sum_recv, raw_send, raw_recv, gram_send,
           gram_recv, back_send, back_recv, acc_send, acc_recv):
    me, mine = lax.axis_index("member"), lax.axis_index("dp")
    rows, width = x_ref.shape
    piece = rows // members
    half = rows // 2
    batch = rows * parts

    def across(t):
        return {"member": me, "dp": flipped(mine, t, parts)}

    def along(i):
        return {"member": lax.rem(me + i, members), "dp": mine}

    def source(i):
        return lax.rem(me + members - i, members)

    def remote(src, dst, send, recv, to):
        return pltpu.make_async_remote_copy(src_ref=src, dst_ref=dst, send_sem=send, recv_sem=recv,
                                            device_id=to, device_id_type=MESH)

    barrier = pltpu.get_barrier_semaphore()
    for t in range(1, parts):
        pl.semaphore_signal(barrier, inc=1, device_id=across(t), device_id_type=MESH)
    for i in range(1, members):
        pl.semaphore_signal(barrier, inc=1, device_id=along(i), device_id_type=MESH)

    sums[0] = jnp.zeros((8, width), jnp.float32)

    @pl.loop(0, rows // 64)
    def _(r):
        block = x_ref[pl.ds(pl.multiple_of(r * 64, 64), 64), :].astype(jnp.float32)
        sums[0] += jnp.sum(block.reshape(8, 8, width), axis=0)

    pl.semaphore_wait(barrier, parts + members - 2)

    sent = []
    sum_copies = []
    for t in range(1, parts):
        copy = remote(sums.at[0], sums.at[t], sum_send.at[t], sum_recv.at[t], across(t))
        copy.start()
        sum_copies.append(copy)
    sent += sum_copies

    relay = parts == 4

    def raw_copy(t, h, src, to):
        at = pl.ds(h * half, half)
        return remote(src.at[at, :], raw.at[t, at, :], raw_send.at[t, h], raw_recv.at[t, h], to)

    raw_copies = {}
    for n in range(2):
        for t in range(1, 3 if relay else parts):
            h = (n + t - 1) % 2
            raw_copies[t, h] = raw_copy(t, h, x_ref, across(t))
            raw_copies[t, h].start()

    for copy in sum_copies:
        copy.wait_recv()
    total = sums[0]
    for t in range(1, parts):
        total = total + sums[t]
    mean = jnp.sum(total, axis=0, keepdims=True) / batch

    gram_copies = []

    def do_part(t):
        @pl.loop(0, rows // 64)
        def _(r):
            at = pl.ds(pl.multiple_of(r * 64, 64), 64)
            block = x_ref[at, :] if t == 0 else raw[t, at, :]
            cent[t, at, :] = (block.astype(jnp.float32) - mean).astype(jnp.bfloat16)

        for n in range(rows // 256):
            gram[t, :, n * 256:(n + 1) * 256] = lax.dot_general(
                cent[0], cent[t, n * 256:(n + 1) * 256, :], (((1,), (1,)), ((), ())),
                preferred_element_type=jnp.float32).astype(jnp.bfloat16)
        for i in range(1, members):
            to = lax.rem(me + i, members)
            copy = remote(gram.at[t, pl.ds(to * piece, piece), :], held.at[me, t],
                          gram_send.at[t, i], gram_recv.at[t, i], along(i))
            copy.start()
            gram_copies.append(copy)
        held[me, t] = gram[t, pl.ds(pl.multiple_of(me * piece, piece), piece), :]

    do_part(0)
    if relay:
        raw_copies[1, 0].wait_recv()
        raw_copies[3, 0] = raw_copy(3, 0, raw.at[1], across(2))
        raw_copies[3, 0].start()
        raw_copies[2, 1].wait_recv()
        raw_copies[3, 1] = raw_copy(3, 1, raw.at[2], across(1))
        raw_copies[3, 1].start()
        raw_copies[1, 1].wait_recv()
        do_part(1)
        raw_copies[2, 0].wait_recv()
        do_part(2)
        raw_copies[3, 0].wait_recv()
        raw_copies[3, 1].wait_recv()
        do_part(3)
    else:
        for t in range(1, parts):
            raw_copies[t, 0].wait_recv()
            raw_copies[t, 1].wait_recv()
            do_part(t)
    sent += list(raw_copies.values()) + gram_copies

    tall = min(piece, 32)
    chunks = [(a, b) for a in range(0, piece, tall) for b in range(0, rows, LANES)]
    per_row = rows // LANES
    acc[...] = jnp.zeros(acc.shape, jnp.float32)
    for t in range(parts):
        for i in range(1, members):
            remote(gram.at[t, pl.ds(0, piece), :], held.at[source(i), t], gram_send.at[t, i],
                   gram_recv.at[t, i], along(i)).wait_recv()

        @pl.loop(0, len(chunks))
        def _(c):
            down = pl.ds(pl.multiple_of((c // per_row) * tall, tall), tall)
            over = pl.ds(pl.multiple_of((c % per_row) * LANES, LANES), LANES)
            tiles = [held[q, t, down, over].astype(jnp.float32) for q in range(members)]
            for o in range(pairs + 1):
                for q in range(members):
                    product = tiles[q] * tiles[(q + o) % members]
                    acc[o, q] += jnp.sum(product.reshape(tall // 8, 8, LANES), axis=0)

    for o in range(pairs + 1):
        stage[0, o] = jnp.sum(acc[o], axis=1)
    small = []
    for t in range(1, parts):
        copy = remote(stage.at[0], stage.at[t], acc_send.at[t], acc_recv.at[t], across(t))
        copy.start()
        small.append(copy)
    for copy in small:
        copy.wait_recv()
    value = stage[0]
    for t in range(1, parts):
        value = value + stage[t]
    stage[parts] = value
    for i in range(1, members):
        copy = remote(stage.at[parts], stage.at[parts + i], acc_send.at[parts + i],
                      acc_recv.at[parts + i], along(i))
        copy.start()
        small.append(copy)
    for copy in small[parts - 1:]:
        copy.wait_recv()
    sent += small
    for i in range(1, members):
        value = value + stage[parts + i]
    hsic = [jnp.broadcast_to(jnp.sum(value[o], axis=1, keepdims=True), (members, LANES))
            for o in range(pairs + 1)]
    column = lax.broadcasted_iota(jnp.int32, (members, LANES), 1)
    row = lax.broadcasted_iota(jnp.int32, (members, LANES), 0)
    scores = jnp.zeros((members, LANES), jnp.float32)
    load = jnp.zeros((members, LANES), jnp.float32)
    for o in range(1, pairs + 1):
        norm = jnp.sqrt(hsic[0] * rolled(hsic[0], -o))
        cka = hsic[o] / norm
        scores = jnp.where(column == o - 1, cka, scores)
        weighted = weight_ref[o - 1] * cka
        load = load + weighted + rolled(weighted, o)
        coefs[o] = 2.0 * weight_ref[o - 1] / norm
    coefs[0] = -2.0 * (load / (hsic[0] + 1e-06))
    own = jnp.sum(jnp.where(row == me, scores, 0.0), axis=0, keepdims=True)
    cka_ref[...] = own[:, :pairs]

    back_copies = []
    for t in range(parts):
        @pl.loop(0, len(chunks))
        def _(c):
            down = pl.ds(pl.multiple_of((c // per_row) * tall, tall), tall)
            over = pl.ds(pl.multiple_of((c % per_row) * LANES, LANES), LANES)
            tiles = [held[q, t, down, over].astype(jnp.float32) for q in range(members)]
            for m in range(members):
                out = coefs[0, m:m + 1, :] * tiles[m]
                for o in range(1, pairs + 1):
                    p, q = (m + o) % members, (m - o) % members
                    out = out + coefs[o, m:m + 1, :] * tiles[p] + coefs[o, q:q + 1, :] * tiles[q]
                mixed[m, t, down, over] = out.astype(jnp.bfloat16)

        for i in range(1, members):
            to = lax.rem(me + i, members)
            copy = remote(mixed.at[to, t], back.at[t, pl.ds(me * piece, piece), :],
                          back_send.at[t, i], back_recv.at[t, i], along(i))
            copy.start()
            back_copies.append(copy)
        back[t, pl.ds(pl.multiple_of(me * piece, piece), piece), :] = mixed[me, t]
    sent += back_copies

    scale = math.sqrt(batch)
    for t in range(parts):
        for i in range(1, members):
            remote(mixed.at[0, t], back.at[t, pl.ds(source(i) * piece, piece), :],
                   back_send.at[t, i], back_recv.at[t, i], along(i)).wait_recv()

        @pl.loop(0, width // 256)
        def _(n):
            over = pl.ds(pl.multiple_of(n * 256, 256), 256)
            part = jnp.dot(back[t], cent[t, :, over], preferred_element_type=jnp.float32)
            if t > 0:
                part = grad_ref[:, over] + part
            if t == parts - 1:
                part = scale * part
            grad_ref[:, over] = part

    for copy in sent:
        copy.wait_send()


def shards(feats, pair_weight):
    rows = feats[0]
    parts, members = lax.axis_size("dp"), lax.axis_size("member")
    count, width = rows.shape
    pairs = pair_weight.shape[1]
    piece = count // members
    weights = jnp.broadcast_to(pair_weight.T[:, :, None], (pairs, members, LANES))
    dma = pltpu.SemaphoreType.DMA
    grad, cka = pl.pallas_call(
        functools.partial(kernel, members, parts, pairs),
        out_shape=(jax.ShapeDtypeStruct((count, width), jnp.float32),
                   jax.ShapeDtypeStruct((1, pairs), jnp.float32)),
        in_specs=[pl.BlockSpec(memory_space=pltpu.VMEM)] * 2,
        out_specs=(pl.BlockSpec(memory_space=pltpu.VMEM),) * 2,
        scratch_shapes=[
            pltpu.VMEM((parts, 8, width), jnp.float32),
            pltpu.VMEM((parts, count, width), jnp.bfloat16),
            pltpu.VMEM((parts, count, width), jnp.bfloat16),
            pltpu.VMEM((parts, count, count), jnp.bfloat16),
            pltpu.VMEM((members, parts, piece, count), jnp.bfloat16),
            pltpu.VMEM((members, parts, piece, count), jnp.bfloat16),
            pltpu.VMEM((parts, count, count), jnp.bfloat16),
            pltpu.VMEM((pairs + 1, members, 8, LANES), jnp.float32),
            pltpu.VMEM((parts + members, pairs + 1, members, LANES), jnp.float32),
            pltpu.VMEM((pairs + 1, members, LANES), jnp.float32),
            dma((parts,)), dma((parts,)),
            dma((parts, 2)), dma((parts, 2)),
            dma((parts, members)), dma((parts, members)),
            dma((parts, members)), dma((parts, members)),
            dma((parts + members,)), dma((parts + members,)),
        ],
        compiler_params=pltpu.CompilerParams(
            collective_id=0, has_side_effects=True, vmem_limit_bytes=60 * 1024 * 1024),
    )(rows, weights)
    return (grad[None], cka)


def solution(mesh):
    return jax.shard_map(
        shards,
        mesh=mesh,
        in_specs=(P("member", "dp", None), P()),
        out_specs=(P("member", "dp", None), P("member", None)),
        check_vma=False,
    )
```

```python
import functools
import math

import jax
import jax.numpy as jnp
from jax import lax
from jax.experimental import pallas as pl
from jax.experimental.pallas import tpu as pltpu
from jax.sharding import PartitionSpec as P

MESH = pl.DeviceIdType.MESH
LANES = 128


def ring(index, count):
    if count != 4:
        return index
    return 2 * (index // 2) + ((index % 2) + (index // 2)) % 2


def rolled(value, steps):
    count = value.shape[0]
    steps %= count
    if steps == 0:
        return value
    return jnp.concatenate([value[count - steps:], value[:count - steps]], axis=0)


def kernel(members, parts, pairs, x_ref, weight_ref, grad_ref, cka_ref, sums, raw, cent, gram, held,
           mixed, back, turned, acc, stage, coefs, sum_send, sum_recv, raw_send, raw_recv, gram_send,
           gram_recv, back_send, back_recv, pass_send, pass_recv, acc_send, acc_recv):
    me = lax.axis_index("member")
    place = ring(lax.axis_index("dp"), parts)
    rows, width = x_ref.shape
    piece = rows // members
    half = rows // 2
    batch = rows * parts
    opposite = parts // 2
    upper = place // opposite

    def across(t):
        return {"member": me, "dp": ring(lax.rem(place + t, parts), parts)}

    def along(i):
        return {"member": lax.rem(me + i, members), "dp": lax.axis_index("dp")}

    def source(i):
        return lax.rem(me + members - i, members)

    def remote(src, dst, send, recv, to):
        return pltpu.make_async_remote_copy(src_ref=src, dst_ref=dst, send_sem=send, recv_sem=recv,
                                            device_id=to, device_id_type=MESH)

    def depth(b):
        return piece // 2 if b == opposite else piece

    def slab(b):
        return pl.ds(b * piece, depth(b))

    barrier = pltpu.get_barrier_semaphore()
    for t in range(1, parts):
        pl.semaphore_signal(barrier, inc=1, device_id=across(t), device_id_type=MESH)
    for i in range(1, members):
        pl.semaphore_signal(barrier, inc=1, device_id=along(i), device_id_type=MESH)

    sums[0] = jnp.zeros((8, width), jnp.float32)

    @pl.loop(0, rows // 64)
    def _(r):
        block = x_ref[pl.ds(pl.multiple_of(r * 64, 64), 64), :].astype(jnp.float32)
        sums[0] += jnp.sum(block.reshape(8, 8, width), axis=0)

    pl.semaphore_wait(barrier, parts + members - 2)

    sent = []
    sum_copies = []
    for t in range(1, parts):
        copy = remote(sums.at[0], sums.at[parts - t], sum_send.at[t], sum_recv.at[parts - t], across(t))
        copy.start()
        sum_copies.append(copy)
    sent += sum_copies

    relay = parts == 4

    def send_raw(t, h, src, slot, to):
        at = pl.ds(h * half, half)
        copy = remote(src.at[at, :], raw.at[slot, at, :], raw_send.at[t, h], raw_recv.at[slot, h], to)
        copy.start()
        sent.append(copy)

    def wait_raw(slot, h):
        at = pl.ds(h * half, half)
        remote(x_ref.at[at, :], raw.at[slot, at, :], raw_send.at[slot, h], raw_recv.at[slot, h],
               across(slot)).wait_recv()

    if relay:
        send_raw(3, 0, x_ref, 1, across(3))
        send_raw(1, 1, x_ref, 3, across(1))
        send_raw(3, 1, x_ref, 1, across(3))
    else:
        for t in range(parts - 1, 0, -1):
            for h in range(2):
                send_raw(t, h, x_ref, parts - t, across(t))

    for copy in sum_copies:
        copy.wait_recv()
    total = sums[0]
    for t in range(1, parts):
        total = total + sums[t]
    mean = jnp.sum(total, axis=0, keepdims=True) / batch

    def centre(t):
        @pl.loop(0, rows // 64)
        def _(r):
            at = pl.ds(pl.multiple_of(r * 64, 64), 64)
            block = x_ref[at, :] if t == 0 else raw[t, at, :]
            cent[t, at, :] = (block.astype(jnp.float32) - mean).astype(jnp.bfloat16)

    def multiply(b):
        centre(b)
        if b == opposite:
            left = cent[upper * opposite, pl.ds(pl.multiple_of(upper * half, half), half), :]
        else:
            left = cent[0]
        other = (1 - upper) * opposite if b == opposite else b
        tall = left.shape[0]
        for n in range(rows // 256):
            gram[b, :tall, n * 256:(n + 1) * 256] = lax.dot_general(
                left, cent[other, n * 256:(n + 1) * 256, :], (((1,), (1,)), ((), ())),
                preferred_element_type=jnp.float32).astype(jnp.bfloat16)
        for i in range(1, members):
            to = lax.rem(me + i, members)
            copy = remote(gram.at[b, pl.ds(to * depth(b), depth(b)), :], held.at[me, slab(b)],
                          gram_send.at[b, i], gram_recv.at[b, i], along(i))
            copy.start()
            sent.append(copy)
        held[me, slab(b)] = gram[b, pl.ds(pl.multiple_of(me * depth(b), depth(b)), depth(b)), :]

    def chunks(b):
        tall = min(depth(b), 32)
        per_row = rows // LANES

        def place_of(c):
            down = pl.ds(pl.multiple_of(b * piece + (c // per_row) * tall, tall), tall)
            return down, pl.ds(pl.multiple_of((c % per_row) * LANES, LANES), LANES)

        return tall, (depth(b) // tall) * per_row, place_of

    def score(b):
        for i in range(1, members):
            remote(gram.at[b, pl.ds(0, depth(b)), :], held.at[source(i), slab(b)], gram_send.at[b, i],
                   gram_recv.at[b, i], along(i)).wait_recv()
        tall, count, place_of = chunks(b)

        @pl.loop(0, count)
        def _(c):
            down, over = place_of(c)
            tiles = [held[q, down, over].astype(jnp.float32) for q in range(members)]
            for o in range(pairs + 1):
                for q in range(members):
                    product = tiles[q] * tiles[(q + o) % members]
                    acc[o, q] += jnp.sum(product.reshape(tall // 8, 8, LANES), axis=0)

    multiply(0)
    if relay:
        wait_raw(1, 0)
        send_raw(2, 0, raw.at[1], 2, across(3))
        wait_raw(3, 1)
        send_raw(2, 1, raw.at[3], 2, across(1))
        send_raw(1, 0, x_ref, 3, across(1))
        wait_raw(1, 1)
    acc[...] = jnp.zeros(acc.shape, jnp.float32)
    for b in range(1, opposite + 1):
        if not relay or b == opposite:
            wait_raw(b, 0)
            wait_raw(b, 1)
        if b == opposite:
            score(0)
            acc[...] = 0.5 * acc[...]
        multiply(b)
    for t in range(opposite + 1, parts):
        if not relay:
            wait_raw(t, 1)
        wait_raw(t, 0)
        centre(t)
    for b in range(1, opposite + 1):
        score(b)

    for o in range(pairs + 1):
        stage[0, o] = 2.0 * jnp.sum(acc[o], axis=1)
    small = []
    for t in range(1, parts):
        copy = remote(stage.at[0], stage.at[parts - t], acc_send.at[t], acc_recv.at[parts - t], across(t))
        copy.start()
        small.append(copy)
    for copy in small:
        copy.wait_recv()
    value = stage[0]
    for t in range(1, parts):
        value = value + stage[t]
    stage[parts] = value
    for i in range(1, members):
        copy = remote(stage.at[parts], stage.at[parts + i], acc_send.at[parts + i],
                      acc_recv.at[parts + i], along(i))
        copy.start()
        small.append(copy)
    for copy in small[parts - 1:]:
        copy.wait_recv()
    sent += small
    everyone = [value] + [stage[parts + i] for i in range(1, members)]
    while len(everyone) > 1:
        everyone = [sum(everyone[n:n + 2]) for n in range(0, len(everyone), 2)]
    hsic = [jnp.broadcast_to(jnp.sum(everyone[0][o], axis=1, keepdims=True), (members, LANES))
            for o in range(pairs + 1)]
    column = lax.broadcasted_iota(jnp.int32, (members, LANES), 1)
    row = lax.broadcasted_iota(jnp.int32, (members, LANES), 0)
    scores = jnp.zeros((members, LANES), jnp.float32)
    load = jnp.zeros((members, LANES), jnp.float32)
    for o in range(1, pairs + 1):
        weight = jnp.broadcast_to(weight_ref[:, o - 1:o], (members, LANES))
        norm = jnp.sqrt(hsic[0] * rolled(hsic[0], -o))
        cka = hsic[o] / norm
        scores = jnp.where(column == o - 1, cka, scores)
        weighted = weight * cka
        load = load + weighted + rolled(weighted, o)
        coefs[o] = 2.0 * weight / norm
    coefs[0] = -2.0 * (load / (hsic[0] + 1e-06))
    own = jnp.sum(jnp.where(row == me, scores, 0.0), axis=0, keepdims=True)
    cka_ref[...] = own[:, :pairs]

    def landing(b, member):
        start = upper * half if b == opposite else 0
        return pl.ds(pl.multiple_of(start + member * depth(b), depth(b)), depth(b))

    def pass_on(b, i):
        if b == 0:
            return
        at = landing(b, source(i))
        copy = remote(back.at[b, at, :], back.at[parts - b, at, :], pass_send.at[b, i],
                      pass_recv.at[b, i], across(b))
        copy.start()
        sent.append(copy)

    def mix(b):
        tall, count, place_of = chunks(b)

        @pl.loop(0, count)
        def _(c):
            down, over = place_of(c)
            tiles = [held[q, down, over].astype(jnp.float32) for q in range(members)]
            for m in range(members):
                out = coefs[0, m:m + 1, :] * tiles[m]
                for o in range(1, pairs + 1):
                    p, q = (m + o) % members, (m - o) % members
                    out = out + coefs[o, m:m + 1, :] * tiles[p] + coefs[o, q:q + 1, :] * tiles[q]
                mixed[m, down, over] = out.astype(jnp.bfloat16)

        for i in range(1, members):
            to = lax.rem(me + i, members)
            copy = remote(mixed.at[to, slab(b)], back.at[b, landing(b, me), :],
                          back_send.at[b, i], back_recv.at[b, i], along(i))
            copy.start()
            sent.append(copy)
        back[b, landing(b, me), :] = mixed[me, slab(b)]
        pass_on(b, 0)

    order = list(range(1, opposite + 1)) + [0]
    for b in order:
        mix(b)

    scale = math.sqrt(batch)

    def add(left, t, first=False, last=False):
        @pl.loop(0, width // 256)
        def _(n):
            over = pl.ds(pl.multiple_of(n * 256, 256), 256)
            part = jnp.dot(left[...], cent[t, :, over], preferred_element_type=jnp.float32)
            if not first:
                part = grad_ref[:, over] + part
            if last:
                part = scale * part
            grad_ref[:, over] = part

    def turn(t):
        turned[...] = back[t].T

    for n, b in enumerate(order):
        for i in range(1, members):
            remote(mixed.at[0, slab(b)], back.at[b, landing(b, source(i)), :], back_send.at[b, i],
                   back_recv.at[b, i], along(i)).wait_recv()
            pass_on(b, i)
        if b != opposite:
            add(back.at[b], b, first=n == 0)
    for b in range(1, opposite + 1):
        far = b == opposite
        for i in range(members):
            start = (1 - upper) * half if far else 0
            at = pl.ds(pl.multiple_of(start + source(i) * depth(b), depth(b)), depth(b))
            remote(back.at[b, pl.ds(0, depth(b)), :], back.at[parts - b, at, :], pass_send.at[b, i],
                   pass_recv.at[b, i], across(b)).wait_recv()
        if far:
            @pl.when(upper == 1)
            def _():
                turn(b)

            @pl.when(upper == 0)
            def _():
                turned[...] = back[b]
        else:
            turn(parts - b)
        add(turned, parts - b, last=far)

    for copy in sent:
        copy.wait_send()


def shards(feats, pair_weight):
    rows = feats[0]
    parts, members = lax.axis_size("dp"), lax.axis_size("member")
    count, width = rows.shape
    pairs = pair_weight.shape[1]
    piece = count // members
    blocks = parts // 2 + 1
    tall = piece * (parts // 2) + piece // 2
    dma = pltpu.SemaphoreType.DMA
    grad, cka = pl.pallas_call(
        functools.partial(kernel, members, parts, pairs),
        out_shape=(jax.ShapeDtypeStruct((count, width), jnp.float32),
                   jax.ShapeDtypeStruct((1, pairs), jnp.float32)),
        in_specs=[pl.BlockSpec(memory_space=pltpu.VMEM)] * 2,
        out_specs=(pl.BlockSpec(memory_space=pltpu.VMEM),) * 2,
        scratch_shapes=[
            pltpu.VMEM((parts, 8, width), jnp.float32),
            pltpu.VMEM((parts, count, width), jnp.bfloat16),
            pltpu.VMEM((parts, count, width), jnp.bfloat16),
            pltpu.VMEM((blocks, count, count), jnp.bfloat16),
            pltpu.VMEM((members, tall, count), jnp.bfloat16),
            pltpu.VMEM((members, tall, count), jnp.bfloat16),
            pltpu.VMEM((parts, count, count), jnp.bfloat16),
            pltpu.VMEM((count, count), jnp.bfloat16),
            pltpu.VMEM((pairs + 1, members, 8, LANES), jnp.float32),
            pltpu.VMEM((parts + members, pairs + 1, members, LANES), jnp.float32),
            pltpu.VMEM((pairs + 1, members, LANES), jnp.float32),
            dma((parts,)), dma((parts,)),
            dma((parts, 2)), dma((parts, 2)),
            dma((blocks, members)), dma((blocks, members)),
            dma((blocks, members)), dma((blocks, members)),
            dma((blocks, members)), dma((blocks, members)),
            dma((parts + members,)), dma((parts + members,)),
        ],
        compiler_params=pltpu.CompilerParams(
            collective_id=0, has_side_effects=True, vmem_limit_bytes=60 * 1024 * 1024),
    )(rows, pair_weight)
    return (grad[None], cka)


def solution(mesh):
    return jax.shard_map(
        shards,
        mesh=mesh,
        in_specs=(P("member", "dp", None), P()),
        out_specs=(P("member", "dp", None), P("member", None)),
        check_vma=False,
    )
```

```python
import functools
import math

import jax
import jax.numpy as jnp
from jax import lax
from jax.experimental import pallas as pl
from jax.experimental.pallas import tpu as pltpu
from jax.sharding import PartitionSpec as P

MESH = pl.DeviceIdType.MESH
LANES = 128


def ring(index, count):
    if count != 4:
        return index
    return 2 * (index // 2) + ((index % 2) + (index // 2)) % 2


def rolled(value, steps):
    count = value.shape[0]
    steps %= count
    if steps == 0:
        return value
    return jnp.concatenate([value[count - steps:], value[:count - steps]], axis=0)


def kernel(members, parts, pairs, x_ref, weight_ref, grad_ref, cka_ref, sums, raw, cent, gram, held,
           mixed, back, middle, turned, acc, stage, coefs, sum_send, sum_recv, raw_send, raw_recv, gram_send,
           gram_recv, back_send, back_recv, pass_send, pass_recv, acc_send, acc_recv):
    me = lax.axis_index("member")
    place = ring(lax.axis_index("dp"), parts)
    rows, width = x_ref.shape
    piece = rows // members
    half = rows // 2
    batch = rows * parts
    opposite = parts // 2
    upper = place // opposite

    def across(t):
        return {"member": me, "dp": ring(lax.rem(place + t, parts), parts)}

    def along(i):
        return {"member": lax.rem(me + i, members), "dp": lax.axis_index("dp")}

    def source(i):
        return lax.rem(me + members - i, members)

    def remote(src, dst, send, recv, to):
        return pltpu.make_async_remote_copy(src_ref=src, dst_ref=dst, send_sem=send, recv_sem=recv,
                                            device_id=to, device_id_type=MESH)

    def depth(b):
        return piece // 2 if b == opposite else piece

    def slab(b):
        return pl.ds(b * piece, depth(b))

    barrier = pltpu.get_barrier_semaphore()
    for t in range(1, parts):
        pl.semaphore_signal(barrier, inc=1, device_id=across(t), device_id_type=MESH)
    for i in range(1, members):
        pl.semaphore_signal(barrier, inc=1, device_id=along(i), device_id_type=MESH)

    sums[0] = jnp.zeros((8, width), jnp.float32)

    @pl.loop(0, rows // 64)
    def _(r):
        block = x_ref[pl.ds(pl.multiple_of(r * 64, 64), 64), :].astype(jnp.float32)
        sums[0] += jnp.sum(block.reshape(8, 8, width), axis=0)

    pl.semaphore_wait(barrier, parts + members - 2)

    sent = []
    sum_copies = []
    for t in range(1, parts):
        copy = remote(sums.at[0], sums.at[parts - t], sum_send.at[t], sum_recv.at[parts - t], across(t))
        copy.start()
        sum_copies.append(copy)
    sent += sum_copies

    relay = parts == 4

    def send_raw(t, h, src, slot, to):
        at = pl.ds(h * half, half)
        copy = remote(src.at[at, :], raw.at[slot, at, :], raw_send.at[t, h], raw_recv.at[slot, h], to)
        copy.start()
        sent.append(copy)

    def wait_raw(slot, h):
        at = pl.ds(h * half, half)
        remote(x_ref.at[at, :], raw.at[slot, at, :], raw_send.at[slot, h], raw_recv.at[slot, h],
               across(slot)).wait_recv()

    if relay:
        send_raw(3, 0, x_ref, 1, across(3))
        send_raw(1, 1, x_ref, 3, across(1))
        send_raw(3, 1, x_ref, 1, across(3))
        send_raw(1, 0, x_ref, 3, across(1))
    else:
        for t in range(parts - 1, 0, -1):
            for h in range(2):
                send_raw(t, h, x_ref, parts - t, across(t))

    for copy in sum_copies:
        copy.wait_recv()
    total = sums[0]
    for t in range(1, parts):
        total = total + sums[t]
    mean = jnp.sum(total, axis=0, keepdims=True) / batch

    def centre(t, h):
        @pl.loop(0, half // 64)
        def _(r):
            at = pl.ds(pl.multiple_of(h * half + r * 64, 64), 64)
            block = x_ref[at, :] if t == 0 else raw[t, at, :]
            cent[t, at, :] = (block.astype(jnp.float32) - mean).astype(jnp.bfloat16)

    turns = ((place + 1) // 2) % 2
    low = 1 + 2 * turns if relay else upper * opposite
    high = 3 - 2 * turns if relay else (1 - upper) * opposite

    def multiply(b, n):
        if b == opposite:
            left = cent[low, pl.ds(pl.multiple_of(upper * half, half), half), :]
        else:
            left = cent[0]
        other = high if b == opposite else b
        tall = left.shape[0]
        over = pl.ds(n * half, half)
        gram[b, :tall, over] = lax.dot_general(
            left, cent[other, over, :], (((1,), (1,)), ((), ())),
            preferred_element_type=jnp.float32).astype(jnp.bfloat16)
        for i in range(1, members):
            to = lax.rem(me + i, members)
            copy = remote(gram.at[b, pl.ds(to * depth(b), depth(b)), over], held.at[me, slab(b), over],
                          gram_send.at[b, n, i], gram_recv.at[b, n, i], along(i))
            copy.start()
            sent.append(copy)
        held[me, slab(b), over] = gram[b, pl.ds(pl.multiple_of(me * depth(b), depth(b)), depth(b)), over]

    def chunks(b):
        tall = min(depth(b), 32)
        per_row = rows // LANES

        def place_of(c):
            down = pl.ds(pl.multiple_of(b * piece + (c // per_row) * tall, tall), tall)
            return down, pl.ds(pl.multiple_of((c % per_row) * LANES, LANES), LANES)

        return tall, (depth(b) // tall) * per_row, place_of

    def score(b):
        for n in range(2):
            over = pl.ds(n * half, half)
            for i in range(1, members):
                remote(gram.at[b, pl.ds(0, depth(b)), over], held.at[source(i), slab(b), over],
                       gram_send.at[b, n, i], gram_recv.at[b, n, i], along(i)).wait_recv()
        tall, count, place_of = chunks(b)

        @pl.loop(0, count)
        def _(c):
            down, over = place_of(c)
            tiles = [held[q, down, over].astype(jnp.float32) for q in range(members)]
            for o in range(pairs + 1):
                for q in range(members):
                    product = tiles[q] * tiles[(q + o) % members]
                    acc[o, q] += jnp.sum(product.reshape(tall // 8, 8, LANES), axis=0)

    for h in range(2):
        centre(0, h)
    for h in range(2):
        multiply(0, h)
    acc[...] = jnp.zeros(acc.shape, jnp.float32)
    if relay:
        wait_raw(1, 0)
        centre(1, 0)
        multiply(1, 0)
        wait_raw(3, 1)
        centre(3, 1)
        score(0)
        acc[...] = 0.5 * acc[...]
        wait_raw(1, 1)
        centre(1, 1)
        multiply(1, 1)
        wait_raw(3, 0)
        send_raw(2, 0, raw.at[1], 2, across(3))
        send_raw(2, 1, raw.at[3], 2, across(1))
        centre(3, 0)
        multiply(2, 0)
        multiply(2, 1)
    else:
        for b in range(1, opposite + 1):
            for h in range(2):
                wait_raw(b, h)
                centre(b, h)
            if b == opposite:
                score(0)
                acc[...] = 0.5 * acc[...]
            multiply(b, 0)
            multiply(b, 1)
        for t in range(opposite + 1, parts):
            for h in range(2):
                wait_raw(t, h)
                centre(t, h)
    for b in range(1, opposite + 1):
        score(b)

    for o in range(pairs + 1):
        stage[0, o] = 2.0 * jnp.sum(acc[o], axis=1)
    small = []
    for t in range(1, parts):
        copy = remote(stage.at[0], stage.at[parts - t], acc_send.at[t], acc_recv.at[parts - t], across(t))
        copy.start()
        small.append(copy)
    for copy in small:
        copy.wait_recv()
    value = stage[0]
    for t in range(1, parts):
        value = value + stage[t]
    stage[parts] = value
    for i in range(1, members):
        copy = remote(stage.at[parts], stage.at[parts + i], acc_send.at[parts + i],
                      acc_recv.at[parts + i], along(i))
        copy.start()
        small.append(copy)
    for copy in small[parts - 1:]:
        copy.wait_recv()
    sent += small
    everyone = [value] + [stage[parts + i] for i in range(1, members)]
    while len(everyone) > 1:
        everyone = [sum(everyone[n:n + 2]) for n in range(0, len(everyone), 2)]
    hsic = [jnp.broadcast_to(jnp.sum(everyone[0][o], axis=1, keepdims=True), (members, LANES))
            for o in range(pairs + 1)]
    column = lax.broadcasted_iota(jnp.int32, (members, LANES), 1)
    row = lax.broadcasted_iota(jnp.int32, (members, LANES), 0)
    scores = jnp.zeros((members, LANES), jnp.float32)
    load = jnp.zeros((members, LANES), jnp.float32)
    for o in range(1, pairs + 1):
        weight = jnp.broadcast_to(weight_ref[:, o - 1:o], (members, LANES))
        norm = jnp.sqrt(hsic[0] * rolled(hsic[0], -o))
        cka = hsic[o] / norm
        scores = jnp.where(column == o - 1, cka, scores)
        weighted = weight * cka
        load = load + weighted + rolled(weighted, o)
        coefs[o] = 2.0 * weight / norm
    coefs[0] = -2.0 * (load / (hsic[0] + 1e-06))
    own = jnp.sum(jnp.where(row == me, scores, 0.0), axis=0, keepdims=True)
    cka_ref[...] = own[:, :pairs]

    def landing(b, member, side=upper):
        start = side * half if b == opposite else 0
        return pl.ds(pl.multiple_of(start + member * depth(b), depth(b)), depth(b))

    def arrival(b):
        return middle if relay and b == opposite else back.at[b]

    def pass_on(b, i):
        if b == 0:
            return
        at = landing(b, source(i))
        for step in (1, 3) if relay and b == opposite else (b,):
            lane = 3 if step == 3 else b
            copy = remote(arrival(b).at[at, :], back.at[parts - b, at, :], pass_send.at[lane, i],
                          pass_recv.at[lane, i], across(step))
            copy.start()
            sent.append(copy)

    def mix(b):
        tall, count, place_of = chunks(b)

        @pl.loop(0, count)
        def _(c):
            down, over = place_of(c)
            tiles = [held[q, down, over].astype(jnp.float32) for q in range(members)]
            for m in range(members):
                out = coefs[0, m:m + 1, :] * tiles[m]
                for o in range(1, pairs + 1):
                    p, q = (m + o) % members, (m - o) % members
                    out = out + coefs[o, m:m + 1, :] * tiles[p] + coefs[o, q:q + 1, :] * tiles[q]
                mixed[m, down, over] = out.astype(jnp.bfloat16)

        for i in range(1, members):
            to = lax.rem(me + i, members)
            copy = remote(mixed.at[to, slab(b)], arrival(b).at[landing(b, me), :],
                          back_send.at[b, i], back_recv.at[b, i], along(i))
            copy.start()
            sent.append(copy)
        arrival(b)[landing(b, me), :] = mixed[me, slab(b)]
        pass_on(b, 0)

    order = list(range(1, opposite + 1)) + [0]
    for b in order:
        mix(b)

    if relay:
        for h in range(2):
            wait_raw(2, h)
            centre(2, h)

    scale = math.sqrt(batch)

    def add(left, t, first=False, last=False):
        @pl.loop(0, width // 256)
        def _(n):
            over = pl.ds(pl.multiple_of(n * 256, 256), 256)
            part = jnp.dot(left[...], cent[t, :, over], preferred_element_type=jnp.float32)
            if not first:
                part = grad_ref[:, over] + part
            if last:
                part = scale * part
            grad_ref[:, over] = part

    def turn(t):
        turned[...] = back[t].T

    for n, b in enumerate(order):
        for i in range(1, members):
            remote(mixed.at[0, slab(b)], arrival(b).at[landing(b, source(i)), :], back_send.at[b, i],
                   back_recv.at[b, i], along(i)).wait_recv()
            pass_on(b, i)
        if b != opposite:
            add(back.at[b], b, first=n == 0)
    for b in range(1, opposite + 1):
        far = b == opposite
        if relay and far:
            sides = [(2, lax.rem(place + 3, 4) // 2), (3, lax.rem(place + 1, 4) // 2)]
        else:
            sides = [(b, 1 - upper)]
        for lane, side in sides:
            for i in range(members):
                at = landing(b, source(i), side)
                remote(back.at[0, pl.ds(0, depth(b)), :], back.at[parts - b, at, :], pass_send.at[lane, i],
                       pass_recv.at[lane, i], across(b)).wait_recv()
        if far:
            @pl.when(upper == 1)
            def _():
                turn(b)

            @pl.when(upper == 0)
            def _():
                turned[...] = back[b]
        else:
            turn(parts - b)
        add(turned, parts - b, last=far)

    for copy in sent:
        copy.wait_send()


def shards(feats, pair_weight):
    rows = feats[0]
    parts, members = lax.axis_size("dp"), lax.axis_size("member")
    count, width = rows.shape
    pairs = pair_weight.shape[1]
    piece = count // members
    blocks = parts // 2 + 1
    tall = piece * (parts // 2) + piece // 2
    dma = pltpu.SemaphoreType.DMA
    grad, cka = pl.pallas_call(
        functools.partial(kernel, members, parts, pairs),
        out_shape=(jax.ShapeDtypeStruct((count, width), jnp.float32),
                   jax.ShapeDtypeStruct((1, pairs), jnp.float32)),
        in_specs=[pl.BlockSpec(memory_space=pltpu.VMEM)] * 2,
        out_specs=(pl.BlockSpec(memory_space=pltpu.VMEM),) * 2,
        scratch_shapes=[
            pltpu.VMEM((parts, 8, width), jnp.float32),
            pltpu.VMEM((parts, count, width), jnp.bfloat16),
            pltpu.VMEM((parts, count, width), jnp.bfloat16),
            pltpu.VMEM((blocks, count, count), jnp.bfloat16),
            pltpu.VMEM((members, tall, count), jnp.bfloat16),
            pltpu.VMEM((members, tall, count), jnp.bfloat16),
            pltpu.VMEM((parts, count, count), jnp.bfloat16),
            pltpu.VMEM((count, count), jnp.bfloat16),
            pltpu.VMEM((count, count), jnp.bfloat16),
            pltpu.VMEM((pairs + 1, members, 8, LANES), jnp.float32),
            pltpu.VMEM((parts + members, pairs + 1, members, LANES), jnp.float32),
            pltpu.VMEM((pairs + 1, members, LANES), jnp.float32),
            dma((parts,)), dma((parts,)),
            dma((parts, 2)), dma((parts, 2)),
            dma((blocks, 2, members)), dma((blocks, 2, members)),
            dma((blocks, members)), dma((blocks, members)),
            dma((blocks + 1, members)), dma((blocks + 1, members)),
            dma((parts + members,)), dma((parts + members,)),
        ],
        compiler_params=pltpu.CompilerParams(
            collective_id=0, has_side_effects=True, vmem_limit_bytes=60 * 1024 * 1024),
    )(rows, pair_weight)
    return (grad[None], cka)


def solution(mesh):
    return jax.shard_map(
        shards,
        mesh=mesh,
        in_specs=(P("member", "dp", None), P()),
        out_specs=(P("member", "dp", None), P("member", None)),
        check_vma=False,
    )
```

```python
import functools
import math

import jax
import jax.numpy as jnp
from jax import lax
from jax.experimental import pallas as pl
from jax.experimental.pallas import tpu as pltpu
from jax.sharding import PartitionSpec as P

MESH = pl.DeviceIdType.MESH
LANES = 128


def ring(index, count):
    if count != 4:
        return index
    return 2 * (index // 2) + ((index % 2) + (index // 2)) % 2


def rolled(value, steps):
    count = value.shape[0]
    steps %= count
    if steps == 0:
        return value
    return jnp.concatenate([value[count - steps:], value[:count - steps]], axis=0)


def kernel(members, parts, pairs, x_ref, weight_ref, grad_ref, cka_ref, sums, raw, cent, gram, held,
           mixed, back, middle, turned, acc, stage, coefs, sum_send, sum_recv, raw_send, raw_recv, gram_send,
           gram_recv, back_send, back_recv, pass_send, pass_recv, acc_send, acc_recv):
    me = lax.axis_index("member")
    place = ring(lax.axis_index("dp"), parts)
    rows, width = x_ref.shape
    piece = rows // members
    half = rows // 2
    batch = rows * parts
    opposite = parts // 2
    upper = place // opposite

    def across(t):
        return {"member": me, "dp": ring(lax.rem(place + t, parts), parts)}

    def along(i):
        return {"member": lax.rem(me + i, members), "dp": lax.axis_index("dp")}

    def source(i):
        return lax.rem(me + members - i, members)

    def remote(src, dst, send, recv, to):
        return pltpu.make_async_remote_copy(src_ref=src, dst_ref=dst, send_sem=send, recv_sem=recv,
                                            device_id=to, device_id_type=MESH)

    def depth(b):
        return piece // 2 if b == opposite else piece

    def slab(b):
        return pl.ds(b * piece, depth(b))

    barrier = pltpu.get_barrier_semaphore()
    for t in range(1, parts):
        pl.semaphore_signal(barrier, inc=1, device_id=across(t), device_id_type=MESH)
    for i in range(1, members):
        pl.semaphore_signal(barrier, inc=1, device_id=along(i), device_id_type=MESH)

    def gather_sum(r, carry):
        block = x_ref[pl.ds(pl.multiple_of(r * 64, 64), 64), :].astype(jnp.float32)
        return carry + jnp.sum(block.reshape(8, 8, width), axis=0)

    partial = lax.fori_loop(0, rows // 64, gather_sum, jnp.zeros((8, width), jnp.float32))
    sums[0] = jnp.sum(partial, axis=0, keepdims=True)

    pl.semaphore_wait(barrier, parts + members - 2)

    sent = []
    sum_copies = []
    for t in range(1, parts):
        copy = remote(sums.at[0], sums.at[parts - t], sum_send.at[t], sum_recv.at[parts - t], across(t))
        copy.start()
        sum_copies.append(copy)
    sent += sum_copies

    relay = parts == 4

    def send_raw(t, h, src, slot, to):
        at = pl.ds(h * half, half)
        copy = remote(src.at[at, :], raw.at[slot, at, :], raw_send.at[t, h], raw_recv.at[slot, h], to)
        copy.start()
        sent.append(copy)

    def wait_raw(slot, h):
        at = pl.ds(h * half, half)
        remote(x_ref.at[at, :], raw.at[slot, at, :], raw_send.at[slot, h], raw_recv.at[slot, h],
               across(slot)).wait_recv()

    if relay:
        send_raw(3, 0, x_ref, 1, across(3))
        send_raw(1, 1, x_ref, 3, across(1))
        send_raw(3, 1, x_ref, 1, across(3))
        send_raw(1, 0, x_ref, 3, across(1))
    else:
        for t in range(parts - 1, 0, -1):
            for h in range(2):
                send_raw(t, h, x_ref, parts - t, across(t))

    for copy in sum_copies:
        copy.wait_recv()
    total = sums[0]
    for t in range(1, parts):
        total = total + sums[t]
    mean = total / batch

    def centre(t, h):
        @pl.loop(0, half // 64)
        def _(r):
            at = pl.ds(pl.multiple_of(h * half + r * 64, 64), 64)
            block = x_ref[at, :] if t == 0 else raw[t, at, :]
            cent[t, at, :] = (block.astype(jnp.float32) - mean).astype(jnp.bfloat16)

    turns = ((place + 1) // 2) % 2
    low = 1 + 2 * turns if relay else upper * opposite
    high = 3 - 2 * turns if relay else (1 - upper) * opposite

    def multiply(b, n):
        if b == opposite:
            left = cent[low, pl.ds(pl.multiple_of(upper * half, half), half), :]
        else:
            left = cent[0]
        other = high if b == opposite else b
        tall = left.shape[0]
        over = pl.ds(n * half, half)
        gram[b, :tall, over] = lax.dot_general(
            left, cent[other, over, :], (((1,), (1,)), ((), ())),
            preferred_element_type=jnp.float32).astype(jnp.bfloat16)
        for i in range(1, members):
            to = lax.rem(me + i, members)
            copy = remote(gram.at[b, pl.ds(to * depth(b), depth(b)), over], held.at[me, slab(b), over],
                          gram_send.at[b, n, i], gram_recv.at[b, n, i], along(i))
            copy.start()
            sent.append(copy)
        held[me, slab(b), over] = gram[b, pl.ds(pl.multiple_of(me * depth(b), depth(b)), depth(b)), over]

    def chunks(b):
        tall = min(depth(b), 32)
        per_row = rows // LANES

        def place_of(c):
            down = pl.ds(pl.multiple_of(b * piece + (c // per_row) * tall, tall), tall)
            return down, pl.ds(pl.multiple_of((c % per_row) * LANES, LANES), LANES)

        return tall, (depth(b) // tall) * per_row, place_of

    def score(b):
        for n in range(2):
            over = pl.ds(n * half, half)
            for i in range(1, members):
                remote(gram.at[b, pl.ds(0, depth(b)), over], held.at[source(i), slab(b), over],
                       gram_send.at[b, n, i], gram_recv.at[b, n, i], along(i)).wait_recv()
        tall, count, place_of = chunks(b)

        @pl.loop(0, count)
        def _(c):
            down, over = place_of(c)
            tiles = [held[q, down, over].astype(jnp.float32) for q in range(members)]
            for o in range(pairs + 1):
                for q in range(members):
                    product = tiles[q] * tiles[(q + o) % members]
                    acc[o, q] += jnp.sum(product.reshape(tall // 8, 8, LANES), axis=0)

    for h in range(2):
        centre(0, h)
    for h in range(2):
        multiply(0, h)
    acc[...] = jnp.zeros(acc.shape, jnp.float32)
    if relay:
        wait_raw(1, 0)
        centre(1, 0)
        multiply(1, 0)
        wait_raw(3, 1)
        centre(3, 1)
        score(0)
        acc[...] = 0.5 * acc[...]
        wait_raw(1, 1)
        centre(1, 1)
        multiply(1, 1)
        wait_raw(3, 0)
        send_raw(2, 0, raw.at[1], 2, across(3))
        send_raw(2, 1, raw.at[3], 2, across(1))
        centre(3, 0)
        multiply(2, 0)
        multiply(2, 1)
    else:
        for b in range(1, opposite + 1):
            for h in range(2):
                wait_raw(b, h)
                centre(b, h)
            if b == opposite:
                score(0)
                acc[...] = 0.5 * acc[...]
            multiply(b, 0)
            multiply(b, 1)
        for t in range(opposite + 1, parts):
            for h in range(2):
                wait_raw(t, h)
                centre(t, h)
    for b in range(1, opposite + 1):
        score(b)

    column = lax.broadcasted_iota(jnp.int32, (members, LANES), 1)
    packed = jnp.zeros((members, LANES), jnp.float32)
    for o in range(pairs + 1):
        lanes = jnp.sum(jnp.sum(acc[o], axis=1), axis=1, keepdims=True)
        packed = jnp.where(column == o, 2.0 * lanes, packed)
    stage[0] = packed
    small = []
    for t in range(1, parts):
        copy = remote(stage.at[0], stage.at[parts - t], acc_send.at[t], acc_recv.at[parts - t], across(t))
        copy.start()
        small.append(copy)
    for copy in small:
        copy.wait_recv()
    value = stage[0]
    for t in range(1, parts):
        value = value + stage[t]
    stage[parts] = value
    for i in range(1, members):
        copy = remote(stage.at[parts], stage.at[parts + i], acc_send.at[parts + i],
                      acc_recv.at[parts + i], along(i))
        copy.start()
        small.append(copy)
    for copy in small[parts - 1:]:
        copy.wait_recv()
    sent += small
    everyone = [value] + [stage[parts + i] for i in range(1, members)]
    while len(everyone) > 1:
        everyone = [sum(everyone[n:n + 2]) for n in range(0, len(everyone), 2)]
    hsic = [jnp.broadcast_to(everyone[0][:, o:o + 1], (members, LANES)) for o in range(pairs + 1)]
    row = lax.broadcasted_iota(jnp.int32, (members, LANES), 0)
    scores = jnp.zeros((members, LANES), jnp.float32)
    load = jnp.zeros((members, LANES), jnp.float32)
    for o in range(1, pairs + 1):
        weight = jnp.broadcast_to(weight_ref[:, o - 1:o], (members, LANES))
        norm = jnp.sqrt(hsic[0] * rolled(hsic[0], -o))
        cka = hsic[o] / norm
        scores = jnp.where(column == o - 1, cka, scores)
        weighted = weight * cka
        load = load + weighted + rolled(weighted, o)
        coefs[o] = 2.0 * weight / norm
    coefs[0] = -2.0 * (load / (hsic[0] + 1e-06))
    own = jnp.sum(jnp.where(row == me, scores, 0.0), axis=0, keepdims=True)
    cka_ref[...] = own[:, :pairs]

    def landing(b, member, side=upper):
        start = side * half if b == opposite else 0
        return pl.ds(pl.multiple_of(start + member * depth(b), depth(b)), depth(b))

    def arrival(b):
        return middle if relay and b == opposite else back.at[b]

    def pass_on(b, i):
        if b == 0:
            return
        at = landing(b, source(i))
        for step in (1, 3) if relay and b == opposite else (b,):
            lane = 3 if step == 3 else b
            copy = remote(arrival(b).at[at, :], back.at[parts - b, at, :], pass_send.at[lane, i],
                          pass_recv.at[lane, i], across(step))
            copy.start()
            sent.append(copy)

    def mix(b):
        tall, count, place_of = chunks(b)

        @pl.loop(0, count)
        def _(c):
            down, over = place_of(c)
            tiles = [held[q, down, over].astype(jnp.float32) for q in range(members)]
            for m in range(members):
                out = coefs[0, m:m + 1, :] * tiles[m]
                for o in range(1, pairs + 1):
                    p, q = (m + o) % members, (m - o) % members
                    out = out + coefs[o, m:m + 1, :] * tiles[p] + coefs[o, q:q + 1, :] * tiles[q]
                mixed[m, down, over] = out.astype(jnp.bfloat16)

        for i in range(1, members):
            to = lax.rem(me + i, members)
            copy = remote(mixed.at[to, slab(b)], arrival(b).at[landing(b, me), :],
                          back_send.at[b, i], back_recv.at[b, i], along(i))
            copy.start()
            sent.append(copy)
        arrival(b)[landing(b, me), :] = mixed[me, slab(b)]
        pass_on(b, 0)

    order = list(range(1, opposite + 1)) + [0]
    for b in order:
        mix(b)

    if relay:
        for h in range(2):
            wait_raw(2, h)
            centre(2, h)

    scale = math.sqrt(batch)

    def add(left, t, first=False, last=False):
        @pl.loop(0, width // 256)
        def _(n):
            over = pl.ds(pl.multiple_of(n * 256, 256), 256)
            part = jnp.dot(left[...], cent[t, :, over], preferred_element_type=jnp.float32)
            if not first:
                part = grad_ref[:, over] + part
            if last:
                part = scale * part
            grad_ref[:, over] = part

    def turn(t):
        turned[...] = back[t].T

    def collect(b):
        for i in range(1, members):
            remote(mixed.at[0, slab(b)], arrival(b).at[landing(b, source(i)), :], back_send.at[b, i],
                   back_recv.at[b, i], along(i)).wait_recv()
            pass_on(b, i)

    for b in order[:-1]:
        collect(b)
        if b != opposite:
            add(back.at[b], b, first=b == 1)
    for b in range(1, opposite + 1):
        far = b == opposite
        if relay and far:
            sides = [(2, lax.rem(place + 3, 4) // 2), (3, lax.rem(place + 1, 4) // 2)]
        else:
            sides = [(b, 1 - upper)]
        for lane, side in sides:
            for i in range(members):
                at = landing(b, source(i), side)
                remote(back.at[0, pl.ds(0, depth(b)), :], back.at[parts - b, at, :], pass_send.at[lane, i],
                       pass_recv.at[lane, i], across(b)).wait_recv()
        if far:
            @pl.when(upper == 1)
            def _():
                turn(b)

            @pl.when(upper == 0)
            def _():
                turned[...] = back[b]
        else:
            turn(parts - b)
        add(turned, parts - b, first=parts == 2)
    collect(0)
    add(back.at[0], 0, last=True)

    for copy in sent:
        copy.wait_send()


def shards(feats, pair_weight):
    rows = feats[0]
    parts, members = lax.axis_size("dp"), lax.axis_size("member")
    count, width = rows.shape
    pairs = pair_weight.shape[1]
    piece = count // members
    blocks = parts // 2 + 1
    tall = piece * (parts // 2) + piece // 2
    dma = pltpu.SemaphoreType.DMA
    grad, cka = pl.pallas_call(
        functools.partial(kernel, members, parts, pairs),
        out_shape=(jax.ShapeDtypeStruct((count, width), jnp.float32),
                   jax.ShapeDtypeStruct((1, pairs), jnp.float32)),
        in_specs=[pl.BlockSpec(memory_space=pltpu.VMEM)] * 2,
        out_specs=(pl.BlockSpec(memory_space=pltpu.VMEM),) * 2,
        scratch_shapes=[
            pltpu.VMEM((parts, 1, width), jnp.float32),
            pltpu.VMEM((parts, count, width), jnp.bfloat16),
            pltpu.VMEM((parts, count, width), jnp.bfloat16),
            pltpu.VMEM((blocks, count, count), jnp.bfloat16),
            pltpu.VMEM((members, tall, count), jnp.bfloat16),
            pltpu.VMEM((members, tall, count), jnp.bfloat16),
            pltpu.VMEM((parts, count, count), jnp.bfloat16),
            pltpu.VMEM((count, count), jnp.bfloat16),
            pltpu.VMEM((count, count), jnp.bfloat16),
            pltpu.VMEM((pairs + 1, members, 8, LANES), jnp.float32),
            pltpu.VMEM((parts + members, members, LANES), jnp.float32),
            pltpu.VMEM((pairs + 1, members, LANES), jnp.float32),
            dma((parts,)), dma((parts,)),
            dma((parts, 2)), dma((parts, 2)),
            dma((blocks, 2, members)), dma((blocks, 2, members)),
            dma((blocks, members)), dma((blocks, members)),
            dma((blocks + 1, members)), dma((blocks + 1, members)),
            dma((parts + members,)), dma((parts + members,)),
        ],
        compiler_params=pltpu.CompilerParams(
            collective_id=0, has_side_effects=True, vmem_limit_bytes=60 * 1024 * 1024),
    )(rows, pair_weight)
    return (grad[None], cka)


def solution(mesh):
    return jax.shard_map(
        shards,
        mesh=mesh,
        in_specs=(P("member", "dp", None), P()),
        out_specs=(P("member", "dp", None), P("member", None)),
        check_vma=False,
    )
```
